32 devices in a mesh: fsdp: 8 (over z, y), refresh: 4 (over x, core).
Axes of the slice: x: 2, y: 2, z: 4, core: 2. Of those that a mesh axis runs over, the one named last changes fastest.
Arguments:
- gradient: bfloat16 [4, 24, 65536], P('refresh', None, 'fsdp'), may hold values from -6 to 6
- owner: int32 [4, 24, 1], P('refresh'), may hold values from 0 to 7; in each aligned block of 24 rows (0 to 23, 24 to 47, ..., all dimensions but the last counted through in order) at most 4 rows name the same one
- rotation: int32 [8], replicated, may hold values from 0 to 3
- left_factor: float32 [4, 32, 256, 256], P('refresh', 'fsdp'), may hold values from -1 to 8, as said below
- right_factor: float32 [4, 32, 256, 256], P('refresh', 'fsdp'), may hold values from -1 to 8, as said below
- left_basis: float32 [4, 32, 256, 256], P('refresh', 'fsdp'), may hold values from -1 to 1, as said below
- right_basis: float32 [4, 32, 256, 256], P('refresh', 'fsdp'), may hold values from -1 to 1, as said below
- moment: float32 [4, 32, 256, 256], P('refresh', 'fsdp'), may hold values from -4 to 4
- second_moment: float32 [4, 32, 256, 256], P('refresh', 'fsdp'), may hold values from 0.05 to 2
Outputs:
- direction: float32 [4, 24, 65536], P('refresh', None, 'fsdp')
- left_factor_new: float32 [4, 32, 256, 256], P('refresh', 'fsdp')
- right_factor_new: float32 [4, 32, 256, 256], P('refresh', 'fsdp')
- left_basis_new: float32 [4, 32, 256, 256], P('refresh', 'fsdp')
- right_basis_new: float32 [4, 32, 256, 256], P('refresh', 'fsdp')
- moment_new: float32 [4, 32, 256, 256], P('refresh', 'fsdp')
- second_moment_new: float32 [4, 32, 256, 256], P('refresh', 'fsdp')
The draws below stay inside these ranges and needn't reach their ends.
Inputs may be any that keep to these rules, and one draw needn't show every extreme that they name: Within each group no owner is named by more than 4 blocks, a bound that some block reaches; some owner is named by at least one block. The state of block b lies in slot s(b) of the steps; the states of slots that no block takes are carried unchanged. `left_factor`: each slot's factor is symmetric positive definite. `right_factor`: each slot's factor is symmetric positive definite. `left_basis`: each slot's basis is orthogonal. `right_basis`: each slot's basis is orthogonal.
All inputs are finite; a program needn't handle non-finite values.
Results may differ from the reference program's by a relative error of at most 0.0003.
Values may be sent and summed in bfloat16 or wider, within the bound.
A program may use at most 64 MiB of HBM per device.

```python
import math
import jax
import jax.numpy as jnp
import numpy as np
from jax import lax

BS = 256
CAP = 4
GROUPS = 4
BLOCKS = 24
SLOTS = 32
N_FSDP = 8
N_REFRESH = 4


def factor_matrix(key, lowest, highest, spread):
    first, second = jax.random.split(key)
    shape = (GROUPS, SLOTS, BS, BS)
    noise = jax.random.normal(first, shape, jnp.float32) * (spread / math.sqrt(2.0 * BS))
    symmetric = noise + jnp.swapaxes(noise, 2, 3)
    diagonal = jnp.exp(jax.random.uniform(second, shape[:3], jnp.float32, math.log(lowest), math.log(highest)))
    return symmetric + diagonal[..., None] * jnp.eye(BS, dtype=jnp.float32)


def basis_matrix(key):
    noise = jax.random.normal(key, (GROUPS, SLOTS, BS, BS), jnp.float32)
    orthogonal, _ = jnp.linalg.qr(noise)
    return orthogonal


def draw_left_factor(key, part):
    return factor_matrix(jax.random.fold_in(key, 11), 1.0, 4.0, 0.4)


def draw_right_factor(key, part):
    return factor_matrix(jax.random.fold_in(key, 23), 1.0, 4.0, 0.4)


def draw_left_basis(key, part):
    return basis_matrix(jax.random.fold_in(key, 37))


def draw_right_basis(key, part):
    return basis_matrix(jax.random.fold_in(key, 41))


def set_ends(drawn, key, smallest, high):
    longest = drawn.shape.index(max(drawn.shape))
    spots = []
    for shift in (0, 1):
        where = [jax.random.randint(jax.random.fold_in(key, axis), (), 0, length) for axis, length in enumerate(drawn.shape)]
        where[longest] = (where[longest] + shift) % drawn.shape[longest]
        spots.append(tuple(where))
    return drawn.at[spots[0]].set(smallest).at[spots[1]].set(high)


def level_of(own_key, dims, shards, low, largest):
    def one(axis_at, parts):
        draws = jax.random.uniform(jax.random.fold_in(jax.random.fold_in(own_key, 6), axis_at), (parts,), jnp.float32, low / len(shards), largest / len(shards))
        return jnp.repeat(jnp.exp(draws), dims[axis_at] // parts).reshape((-1,) + (1,) * (len(dims) - axis_at - 1))

    loudness = one(*shards[0])
    for cut in shards[1:]:
        loudness = loudness * one(*cut)
    return loudness


def shared_out(own_key, own, number, rows, count, top, most, skew):
    sequence = jax.random.permutation(own_key, count)
    packed, common = portions_of(count, rows * top, most, skew, True), portions_of(count, rows * top, most, skew, False)
    places = jnp.arange(count)

    def named(sizes, turn):
        used = int((sizes > 0).sum())
        fixed = max(1, used // 4)
        moved = fixed + (places - fixed + turn * (used - fixed)) % max(1, count - fixed)
        return jnp.zeros((count,), jnp.int32).at[sequence[jnp.where(places < fixed, places, moved)]].set(jnp.asarray(sizes, jnp.int32))

    sizes = jnp.where(number % 4 == 0, named(packed, number // 4), named(common, number - number // 4 - 1))
    mixed = jax.random.permutation(jax.random.fold_in(own, 3), count)
    donor, taker = mixed[0:count // 2 * 2:2], mixed[1:count // 2 * 2:2]
    margin = jnp.minimum(sizes[donor] - 1, most - sizes[taker]) // 2
    margin = jnp.where((donor == sequence[0]) | (taker == sequence[0]) | (sizes[taker] == 0), 0, jnp.maximum(margin, 0))
    moved = jax.random.randint(jax.random.fold_in(own, 4), (count // 2,), 0, 1 << 20) % (margin + 1)
    sizes = sizes.at[donor].add(-moved).at[taker].add(moved)
    items = jnp.searchsorted(jnp.cumsum(sizes), jnp.arange(rows * top), side="right").astype(jnp.int32)
    table = items.reshape(top, rows).T
    table = table[jax.random.permutation(jax.random.fold_in(own, 1), rows)]
    turn = jax.random.randint(jax.random.fold_in(own, 2), (rows, 1), 0, top)
    return jnp.take_along_axis(table, (jnp.arange(top)[None, :] + turn) % top, axis=1)


def portions_of(amount, total, bound, slope, full):
    loads = [(1 << 20) // math.isqrt(rank ** slope) + 1 for rank in range(1, amount + 1)]
    largest = bound if full else min(bound, max(-(-total // amount), total * loads[0] // sum(loads)))
    least = 1 if total - largest >= amount - 1 else 0
    holding, surplus = [largest] + [least] * (amount - 1), total - largest - least * (amount - 1)
    while surplus > 0:
        free = [i for i in range(1, amount) if holding[i] < largest] or [i for i in range(1, amount) if holding[i] < bound]
        mass, left = sum([loads[i] for i in free]), surplus
        for i in free:
            more = min(bound - holding[i], max(1, left * loads[i] // mass), surplus)
            holding[i] = holding[i] + more
            surplus = surplus - more
    return np.array(holding)


def centred(rng, shape, width, bound, pieces=(), kind=jnp.bfloat16):
    drawn = width * jax.random.normal(rng, shape, jnp.float32)
    if pieces:
        drawn = drawn * level_of(rng, shape, pieces, -0.22, 0.18)
    return jnp.clip(drawn, -bound, bound).astype(kind)


def setup_inputs(seed: int = 0) -> dict:
    streams_of = jax.random.split(jax.random.key(seed), 10)
    gradient = centred(streams_of[0], (GROUPS, BLOCKS, BS * BS), 1.0, 6.0, ((0, 4), (2, 8)))
    owner_keys = jax.random.split(jax.random.fold_in(streams_of[1], 1), GROUPS * BLOCKS // BLOCKS)
    owner_turns = jax.random.permutation(jax.random.fold_in(streams_of[1], 3), GROUPS * BLOCKS // BLOCKS)
    owner = jax.vmap(lambda own, number: shared_out(jax.random.fold_in(streams_of[1], 2), own, number, BLOCKS, N_FSDP, 1, CAP, 1))(owner_keys, owner_turns).reshape((GROUPS, BLOCKS, 1))
    rotation = set_ends(jax.random.randint(streams_of[2], (N_FSDP,), 0, N_REFRESH), jax.random.fold_in(streams_of[2], 1), 0, N_REFRESH - 1).astype(jnp.int32)
    left_factor = draw_left_factor(jax.random.fold_in(streams_of[9], 71), 0)
    right_factor = draw_right_factor(jax.random.fold_in(streams_of[9], 71), 0)
    left_basis = draw_left_basis(jax.random.fold_in(streams_of[9], 71), 0)
    right_basis = draw_right_basis(jax.random.fold_in(streams_of[9], 71), 0)
    moment = centred(streams_of[7], (GROUPS, SLOTS, BS, BS), 0.5, 4.0, ((0, 4), (1, 8)), jnp.float32)
    second_moment = jnp.clip(jnp.exp(math.log(2.0) - 3.6888794 * jax.random.uniform(streams_of[8], (GROUPS, SLOTS, BS, BS), jnp.float32) ** level_of(streams_of[8], (GROUPS, SLOTS, BS, BS), ((0, 4), (1, 8)), -0.2, 0.2)), 0.05, 2.0)
    return dict(gradient=gradient, owner=owner, rotation=rotation, left_factor=left_factor, right_factor=right_factor, left_basis=left_basis, right_basis=right_basis, moment=moment, second_moment=second_moment)


HIGHEST = lax.Precision.HIGHEST
EPSILON = 1e-08

def slot_rows(owners):
    onehot = (owners[:, None] == jnp.arange(N_FSDP, dtype=jnp.int32)[None, :]).astype(jnp.int32)
    before = jnp.cumsum(onehot, axis=0) - onehot
    return (owners * CAP + lax.optimization_barrier(jnp.sum(before * onehot, axis=1))).astype(jnp.int32)

def power_step(factor, basis):
    image = jnp.einsum('sij,sjk->sik', factor, basis, precision=HIGHEST)
    gram = jnp.einsum('sji,sjk->sik', image, image, precision=HIGHEST)
    lower = jnp.linalg.cholesky(gram)
    solved = jax.scipy.linalg.solve_triangular(lower, jnp.swapaxes(image, 1, 2), lower=True)
    return jnp.swapaxes(solved, 1, 2)

def reference(gradient, owner, rotation, left_factor, right_factor, left_basis, right_basis, moment, second_moment):
    target = jax.vmap(slot_rows)(owner[:, :, 0])
    rows = jnp.arange(GROUPS, dtype=jnp.int32)[:, None]
    slotted = jnp.zeros((GROUPS, SLOTS, BS * BS), jnp.bfloat16).at[rows, target].set(gradient)
    live = jnp.zeros((GROUPS, SLOTS), jnp.bool_).at[rows, target].set(True)
    keep = live[:, :, None, None]
    wide = slotted.reshape(GROUPS, SLOTS, BS, BS).astype(jnp.float32)
    gram_left = jnp.einsum('gsij,gskj->gsik', wide, wide, precision=HIGHEST)
    gram_right = jnp.einsum('gsji,gsjk->gsik', wide, wide, precision=HIGHEST)
    left_new = 0.95 * left_factor + 0.05 / BS * gram_left
    right_new = 0.95 * right_factor + 0.05 / BS * gram_right
    moment_next = 0.9 * moment + 0.1 * wide

    def rotate(middle):
        inner = jnp.einsum('gsji,gsjk->gsik', left_basis, middle, precision=HIGHEST)
        return jnp.einsum('gsij,gsjk->gsik', inner, right_basis, precision=HIGHEST)
    turned = rotate(wide)
    turned_moment = rotate(moment_next)
    second_next = 0.95 * second_moment + 0.05 * turned * turned
    scaled = turned_moment / (jnp.sqrt(second_next) + EPSILON)
    backed = jnp.einsum('gsij,gsjk->gsik', left_basis, scaled, precision=HIGHEST)
    update = jnp.einsum('gsij,gskj->gsik', backed, right_basis, precision=HIGHEST)
    direction = update.reshape(GROUPS, SLOTS, BS * BS)[rows, target]
    owner_index = jnp.arange(N_FSDP, dtype=jnp.int32)
    first_slot = (owner_index * CAP).astype(jnp.int32)
    chosen = rotation.astype(jnp.int32)
    fresh_left = power_step(left_new[chosen, first_slot], left_basis[chosen, first_slot])
    fresh_right = power_step(right_new[chosen, first_slot], right_basis[chosen, first_slot])
    fresh_left = jnp.repeat(fresh_left, CAP, axis=0)
    fresh_right = jnp.repeat(fresh_right, CAP, axis=0)
    slot_index = jnp.arange(SLOTS, dtype=jnp.int32)
    slot_chosen = chosen[slot_index // CAP]
    leading = slot_index % CAP == 0
    picked = ((jnp.arange(GROUPS, dtype=jnp.int32)[:, None] == slot_chosen[None, :]) & leading[None, :])[:, :, None, None] & keep
    left_basis_new = jnp.where(picked, fresh_left[None], left_basis)
    right_basis_new = jnp.where(picked, fresh_right[None], right_basis)
    return (direction, jnp.where(keep, left_new, left_factor), jnp.where(keep, right_new, right_factor), left_basis_new, right_basis_new, jnp.where(keep, moment_next, moment), jnp.where(keep, second_next, second_moment))
```

```python
import functools
import jax
import jax.numpy as jnp
from jax import lax
from jax.experimental import pallas as pl
from jax.experimental.pallas import tpu as pltpu
from jax.sharding import PartitionSpec as P

HIGHEST = lax.Precision.HIGHEST
EPSILON = 1e-08
NN = (((1,), (0,)), ((), ()))
TN = (((0,), (0,)), ((), ()))
NT = (((1,), (1,)), ((), ()))


def dot(a, b, dims):
    return lax.dot_general(a, b, dims, preferred_element_type=jnp.float32)


def exact(a, b, dims):
    return lax.dot_general(a, b, dims, precision=HIGHEST, preferred_element_type=jnp.float32)


def split(x):
    high = x.astype(jnp.bfloat16)
    return high, (x - high.astype(jnp.float32)).astype(jnp.bfloat16)


def dot3(a, b, dims):
    return dot(a[0], b[0], dims) + (dot(a[0], b[1], dims) + dot(a[1], b[0], dims))


def moment_kernel(left_ref, right_ref, moment_ref, out_ref):
    inner = dot3(split(left_ref[0]), split(moment_ref[0]), TN)
    out_ref[0] = 0.9 * dot3(split(inner), split(right_ref[0]), NN)


def slot_kernel(
    count_ref,
    blocks_ref,
    lf_ref,
    rf_ref,
    lb_ref,
    rb_ref,
    moment_ref,
    second_ref,
    turned_ref,
    update_ref,
    lf_out,
    rf_out,
    moment_out,
    second_out,
):
    width = lf_ref.shape[1]
    live = pl.program_id(0) < count_ref[0]
    block = blocks_ref[:, 0].reshape(width, width)
    wide = block.astype(jnp.float32)
    scale = 0.05 / width
    lf = lf_ref[0]
    rf = rf_ref[0]
    lf_out[0] = jnp.where(live, 0.95 * lf + scale * dot(block, block, NT), lf)
    rf_out[0] = jnp.where(live, 0.95 * rf + scale * dot(block, block, TN), rf)
    moment = moment_ref[0]
    moment_out[0] = jnp.where(live, 0.9 * moment + 0.1 * wide, moment)
    left = split(lb_ref[0])
    right = split(rb_ref[0])
    inner = dot(left[0], block, TN) + dot(left[1], block, TN)
    turned = dot3(split(inner), right, NN)
    second = second_ref[0]
    second_next = 0.95 * second + 0.05 * turned * turned
    second_out[0] = jnp.where(live, second_next, second)
    turned_moment = turned_ref[0] + 0.1 * turned
    scaled = turned_moment / (jnp.sqrt(second_next) + EPSILON)
    backed = dot3(left, split(scaled), NN)
    update = dot3(split(backed), right, NT)
    update_ref[:, 0] = update.reshape(update_ref.shape[0], update_ref.shape[2], width)


def eliminate(tiles, size, group):
    count = len(tiles)
    rows_of = lax.broadcasted_iota(jnp.int32, tiles[0][0].shape, 0)
    inverses = [[jnp.zeros_like(t) for t in tiles[0]] for _ in range(count)]
    for j in range(0, size, group):
        first = j // 8
        cols = []
        rows = []
        for m in range(count):
            cols.append(
                [
                    [
                        jnp.broadcast_to(t[:, j + k : j + k + 1], t.shape)
                        for t in tiles[m][first:]
                    ]
                    for k in range(group)
                ]
            )
            rows.append(
                [tiles[m][first][(j + k) % 8 : (j + k) % 8 + 1, :] for k in range(group)]
            )
        for k in range(group):
            s = (j + k) % 8
            for m in range(count):
                col = cols[m][k]
                inverse = 1.0 / col[0][s : s + 1, :]
                inverses[m][first] = jnp.where(rows_of == s, inverse, inverses[m][first])
                row = rows[m][k] * inverse
                below = [jnp.where(rows_of > s, col[0], 0.0)] + col[1:]
                for l in range(k + 1, group):
                    at = (j + l) % 8
                    entry = col[0][at : at + 1, :]
                    weight = entry * inverse
                    cols[m][l] = [c - b * weight for c, b in zip(cols[m][l], below)]
                    rows[m][l] = rows[m][l] - entry * row
                for n, b in enumerate(below):
                    tiles[m][first + n] = tiles[m][first + n] - b * row
    return tiles, inverses


def refresh_kernel(
    flag_ref, lf_ref, rf_ref, lb_ref, rb_ref, lb_out, rb_out, work_ref, done_ref, *, size, group
):
    width = lf_ref.shape[1]
    lb_out[...] = lb_ref[...]
    rb_out[...] = rb_ref[...]

    @pl.when(flag_ref[0] > 0)
    def _():
        for m, (factor, basis) in enumerate(((lf_ref, lb_ref), (rf_ref, rb_ref))):
            image = exact(factor[0], basis[0], NN)
            turned = image.T
            work_ref[m, :, :width] = exact(turned, image, NN)
            work_ref[m, :, width:] = turned
        lanes = 2 * size
        lane = lax.broadcasted_iota(jnp.int32, (size, lanes), 1)
        sub = lax.broadcasted_iota(jnp.int32, (size, lanes), 0)
        identity = jnp.where(lane == sub + size, 1.0, 0.0)
        for i in range(width // size):
            low = i * size
            start = low // lanes * lanes
            tiles = []
            for m in range(2):
                part = work_ref[m, low : low + size, start : start + lanes]
                if low != start:
                    part = pltpu.roll(part, size, 1)
                both = jnp.where(lane < size, part, identity)
                tiles.append([both[8 * t : 8 * t + 8, :] for t in range(size // 8)])
            tiles, inverses = eliminate(tiles, size, group)
            for m in range(2):
                inverse_lower = jnp.concatenate(tiles[m], axis=0)[:, size:]
                inverse = jnp.concatenate(inverses[m], axis=0)
                inverse = jnp.concatenate([inverse] * (2 * width // lanes), axis=1)
                solved = exact(inverse_lower, work_ref[m, low : low + size, :], NN)
                done_ref[m, low : low + size, :] = solved[:, width:] * jnp.sqrt(inverse[:, width:])
                if low + size < width:
                    trail = exact(solved[:, :width], solved * inverse, TN)
                    work_ref[m, low + size :, :] -= trail[low + size :, :]
        lb_out[0] = done_ref[0].T
        rb_out[0] = done_ref[1].T


def slot_spec(width):
    return pl.BlockSpec((1, width, width), lambda s: (s, 0, 0))


def body(
    gradient,
    owner,
    rotation,
    left_factor,
    right_factor,
    left_basis,
    right_basis,
    moment,
    second_moment,
):
    shards = lax.axis_size("fsdp")
    mine = lax.axis_index("fsdp")
    group = lax.axis_index("refresh")
    cap = left_factor.shape[1]
    width = left_factor.shape[2]
    rows = width // shards
    f32 = jnp.float32
    owners = owner[0, :, 0]
    onehot = (owners[:, None] == jnp.arange(shards, dtype=jnp.int32)[None, :]).astype(jnp.int32)
    before = jnp.cumsum(onehot, axis=0) - onehot
    target = owners * cap + jnp.sum(before * onehot, axis=1)
    placing = (target[None, :] == jnp.arange(shards * cap, dtype=jnp.int32)[:, None]).astype(
        jnp.bfloat16
    )
    outgoing = jnp.dot(placing, gradient[0], preferred_element_type=f32).astype(jnp.bfloat16)
    outgoing = outgoing.reshape(shards, cap, rows, width)
    arrived = lax.all_to_all(outgoing, "fsdp", split_axis=0, concat_axis=0, tiled=True)
    count = jnp.sum((owners == mine).astype(jnp.int32))
    state = jax.ShapeDtypeStruct((cap, width, width), f32)
    spec = slot_spec(width)
    piece = pl.BlockSpec((shards, 1, rows, width), lambda s: (0, s, 0, 0))
    cube = width * width * width
    turned_old = pl.pallas_call(
        moment_kernel,
        grid=(cap,),
        in_specs=[spec] * 3,
        out_specs=spec,
        out_shape=state,
        cost_estimate=pl.CostEstimate(
            flops=12 * cap * cube, bytes_accessed=16 * cap * width * width, transcendentals=0
        ),
        name="moment_turn",
    )(left_basis[0], right_basis[0], moment[0])
    smem = pl.BlockSpec(memory_space=pltpu.SMEM)
    update, left_new, right_new, moment_new, second_new = pl.pallas_call(
        slot_kernel,
        grid=(cap,),
        in_specs=[smem, piece] + [spec] * 7,
        out_specs=[piece] + [spec] * 4,
        out_shape=[jax.ShapeDtypeStruct((shards, cap, rows, width), f32)] + [state] * 4,
        cost_estimate=pl.CostEstimate(
            flops=26 * cap * cube, bytes_accessed=50 * cap * width * width, transcendentals=0
        ),
        name="slot_step",
    )(
        count.reshape(1),
        arrived,
        left_factor[0],
        right_factor[0],
        left_basis[0],
        right_basis[0],
        moment[0],
        second_moment[0],
        turned_old,
    )
    returned = lax.all_to_all(update, "fsdp", split_axis=0, concat_axis=0, tiled=True)
    chosen = lax.dynamic_index_in_dim(rotation, mine, 0, keepdims=False)
    flag = ((count > 0) & (group == chosen)).astype(jnp.int32).reshape(1)
    size = width // 4 if width % 4 == 0 and width >= 256 else width
    head = pl.BlockSpec((1, width, width), lambda s: (0, 0, 0))
    whole = pl.BlockSpec((cap, width, width), lambda s: (0, 0, 0))
    left_basis_new, right_basis_new = pl.pallas_call(
        functools.partial(refresh_kernel, size=size, group=4),
        grid=(1,),
        in_specs=[smem, head, head, whole, whole],
        out_specs=[whole] * 2,
        out_shape=[state] * 2,
        scratch_shapes=[
            pltpu.VMEM((2, width, 2 * width), f32),
            pltpu.VMEM((2, width, width), f32),
        ],
        cost_estimate=pl.CostEstimate(
            flops=1200 * cube, bytes_accessed=16 * cap * width * width, transcendentals=0
        ),
        name="refresh_step",
    )(flag, left_new, right_new, left_basis[0], right_basis[0])
    direction = jnp.take(returned.reshape(shards * cap, rows, width), target, axis=0)
    direction = direction.reshape(1, target.shape[0], rows * width)
    return (
        direction,
        left_new[None],
        right_new[None],
        left_basis_new[None],
        right_basis_new[None],
        moment_new[None],
        second_new[None],
    )


def solution(mesh):
    state = P("refresh", "fsdp", None, None)
    spread = P("refresh", None, "fsdp")
    in_specs = (spread, P("refresh", None, None), P()) + (state,) * 6
    out_specs = (spread,) + (state,) * 6
    return jax.shard_map(body, mesh=mesh, in_specs=in_specs, out_specs=out_specs, check_vma=False)
```

```python
import functools
import jax
import jax.numpy as jnp
from jax import lax
from jax.experimental import pallas as pl
from jax.experimental.pallas import tpu as pltpu
from jax.sharding import PartitionSpec as P

HIGHEST = lax.Precision.HIGHEST
EPSILON = 1e-08
NN = (((1,), (0,)), ((), ()))
TN = (((0,), (0,)), ((), ()))
NT = (((1,), (1,)), ((), ()))


def dot(a, b, dims):
    return lax.dot_general(a, b, dims, preferred_element_type=jnp.float32)


def exact(a, b, dims):
    return lax.dot_general(a, b, dims, precision=HIGHEST, preferred_element_type=jnp.float32)


def split(x):
    high = x.astype(jnp.bfloat16)
    return high, (x - high.astype(jnp.float32)).astype(jnp.bfloat16)


def dot3(a, b, dims):
    return dot(a[0], b[0], dims) + (dot(a[0], b[1], dims) + dot(a[1], b[0], dims))


def far_first(shards):
    return sorted(range(1, shards), key=lambda d: abs(2 * d - shards))


def greet(shards):
    me = lax.axis_index("fsdp")
    barrier = pltpu.get_barrier_semaphore()
    for d in range(1, shards):
        pl.semaphore_signal(
            barrier,
            inc=1,
            device_id={"fsdp": lax.rem(me + d, shards)},
            device_id_type=pl.DeviceIdType.MESH,
        )
    pl.semaphore_wait(barrier, shards - 1)


def exchange(shards, source, target, send_sem, recv_sem):
    me = lax.axis_index("fsdp")
    copies = []
    for d in far_first(shards):
        peer = lax.rem(me + d, shards)
        copies.append(
            pltpu.make_async_remote_copy(
                src_ref=source.at[peer],
                dst_ref=target.at[me],
                send_sem=send_sem.at[d],
                recv_sem=recv_sem.at[d],
                device_id={"fsdp": peer},
                device_id_type=pl.DeviceIdType.MESH,
            )
        )
    copies.append(pltpu.make_async_copy(source.at[me], target.at[me], send_sem.at[0]))
    for copy in copies:
        copy.start()
    return copies


def send_kernel(
    shards,
    out_ref,
    left_ref,
    right_ref,
    moment_ref,
    arrived_ref,
    turned_ref,
    state_ref,
    send_sem,
    recv_sem,
    load_sem,
):
    loads = [
        pltpu.make_async_copy(ref, state_ref.at[i], load_sem.at[i])
        for i, ref in enumerate((left_ref, moment_ref, right_ref))
    ]
    for load in loads:
        load.start()
    greet(shards)
    copies = exchange(shards, out_ref, arrived_ref, send_sem, recv_sem)
    for load in loads:
        load.wait()
    for s in range(turned_ref.shape[0]):
        inner = dot3(split(state_ref[0, s]), split(state_ref[1, s]), TN)
        turned_ref[s] = 0.9 * dot3(split(inner), split(state_ref[2, s]), NN)
    for copy in copies:
        copy.wait()


def slot_kernel(
    count_ref,
    blocks_ref,
    lf_ref,
    rf_ref,
    lb_ref,
    rb_ref,
    moment_ref,
    second_ref,
    turned_ref,
    update_ref,
    lf_out,
    rf_out,
    moment_out,
    second_out,
    lb_out,
    rb_out,
):
    lb_out[0] = lb_ref[0]
    rb_out[0] = rb_ref[0]
    width = lf_ref.shape[1]
    live = pl.program_id(0) < count_ref[0]
    block = blocks_ref[:, 0].reshape(width, width)
    wide = block.astype(jnp.float32)
    scale = 0.05 / width
    lf = lf_ref[0]
    rf = rf_ref[0]
    lf_out[0] = jnp.where(live, 0.95 * lf + scale * dot(block, block, NT), lf)
    rf_out[0] = jnp.where(live, 0.95 * rf + scale * dot(block, block, TN), rf)
    moment = moment_ref[0]
    moment_out[0] = jnp.where(live, 0.9 * moment + 0.1 * wide, moment)
    left = split(lb_ref[0])
    right = split(rb_ref[0])
    inner = dot(left[0], block, TN) + dot(left[1], block, TN)
    turned = dot3(split(inner), right, NN)
    second = second_ref[0]
    second_next = 0.95 * second + 0.05 * turned * turned
    second_out[0] = jnp.where(live, second_next, second)
    turned_moment = turned_ref[0] + 0.1 * turned
    scaled = turned_moment / (jnp.sqrt(second_next) + EPSILON)
    backed = dot3(left, split(scaled), NN)
    update = dot3(split(backed), right, NT)
    update_ref[:, 0] = update.reshape(update_ref.shape[0], update_ref.shape[2], width)


def eliminate(tiles, size, group):
    count = len(tiles)
    rows_of = lax.broadcasted_iota(jnp.int32, tiles[0][0].shape, 0)
    inverses = [[jnp.zeros_like(t) for t in tiles[0]] for _ in range(count)]
    for j in range(0, size, group):
        first = j // 8
        cols = []
        rows = []
        for m in range(count):
            cols.append(
                [
                    [
                        jnp.broadcast_to(t[:, j + k : j + k + 1], t.shape)
                        for t in tiles[m][first:]
                    ]
                    for k in range(group)
                ]
            )
            rows.append(
                [tiles[m][first][(j + k) % 8 : (j + k) % 8 + 1, :] for k in range(group)]
            )
        for k in range(group):
            s = (j + k) % 8
            for m in range(count):
                col = cols[m][k]
                inverse = 1.0 / col[0][s : s + 1, :]
                inverses[m][first] = jnp.where(rows_of == s, inverse, inverses[m][first])
                row = rows[m][k] * inverse
                below = [jnp.where(rows_of > s, col[0], 0.0)] + col[1:]
                for l in range(k + 1, group):
                    at = (j + l) % 8
                    entry = col[0][at : at + 1, :]
                    weight = entry * inverse
                    cols[m][l] = [c - b * weight for c, b in zip(cols[m][l], below)]
                    rows[m][l] = rows[m][l] - entry * row
                for n, b in enumerate(below):
                    tiles[m][first + n] = tiles[m][first + n] - b * row
    return tiles, inverses


def return_kernel(
    shards,
    size,
    group,
    update_ref,
    lf_ref,
    rf_ref,
    lb_ref,
    rb_ref,
    returned_ref,
    lb_out,
    rb_out,
    work_ref,
    done_ref,
    send_sem,
    recv_sem,
):
    width = lf_ref.shape[1]
    greet(shards)
    copies = exchange(shards, update_ref, returned_ref, send_sem, recv_sem)
    for m, (factor, basis) in enumerate(((lf_ref, lb_ref), (rf_ref, rb_ref))):
        image = exact(factor[0], basis[0], NN)
        turned = image.T
        work_ref[m, :, :width] = exact(turned, image, NN)
        work_ref[m, :, width:] = turned
    lanes = 2 * size
    lane = lax.broadcasted_iota(jnp.int32, (size, lanes), 1)
    sub = lax.broadcasted_iota(jnp.int32, (size, lanes), 0)
    identity = jnp.where(lane == sub + size, 1.0, 0.0)
    for i in range(width // size):
        low = i * size
        start = low // lanes * lanes
        tiles = []
        for m in range(2):
            part = work_ref[m, low : low + size, start : start + lanes]
            if low != start:
                part = pltpu.roll(part, size, 1)
            both = jnp.where(lane < size, part, identity)
            tiles.append([both[8 * t : 8 * t + 8, :] for t in range(size // 8)])
        tiles, inverses = eliminate(tiles, size, group)
        for m in range(2):
            inverse_lower = jnp.concatenate(tiles[m], axis=0)[:, size:]
            inverse = jnp.concatenate(inverses[m], axis=0)
            inverse = jnp.concatenate([inverse] * (2 * width // lanes), axis=1)
            solved = exact(inverse_lower, work_ref[m, low : low + size, :], NN)
            done_ref[m, low : low + size, :] = solved[:, width:] * jnp.sqrt(inverse[:, width:])
            if low + size < width:
                trail = exact(solved[:, :width], solved * inverse, TN)
                work_ref[m, low + size :, :] -= trail[low + size :, :]
    lb_out[...] = done_ref[0].T
    rb_out[...] = done_ref[1].T
    for copy in copies:
        copy.wait()


def place_kernel(flag_ref, left_ref, right_ref, lb_ref, rb_ref, lb_out, rb_out):
    fresh = flag_ref[0] > 0
    lb_out[0] = jnp.where(fresh, left_ref[...], lb_ref[0])
    rb_out[0] = jnp.where(fresh, right_ref[...], rb_ref[0])


def slot_spec(width):
    return pl.BlockSpec((1, width, width), lambda s: (s, 0, 0))


def body(
    gradient,
    owner,
    rotation,
    left_factor,
    right_factor,
    left_basis,
    right_basis,
    moment,
    second_moment,
):
    shards = lax.axis_size("fsdp")
    mine = lax.axis_index("fsdp")
    group = lax.axis_index("refresh")
    cap = left_factor.shape[1]
    width = left_factor.shape[2]
    rows = width // shards
    f32 = jnp.float32
    owners = owner[0, :, 0]
    onehot = (owners[:, None] == jnp.arange(shards, dtype=jnp.int32)[None, :]).astype(jnp.int32)
    before = jnp.cumsum(onehot, axis=0) - onehot
    target = owners * cap + jnp.sum(before * onehot, axis=1)
    placing = (target[None, :] == jnp.arange(shards * cap, dtype=jnp.int32)[:, None]).astype(
        jnp.bfloat16
    )
    outgoing = jnp.dot(placing, gradient[0], preferred_element_type=f32).astype(jnp.bfloat16)
    outgoing = outgoing.reshape(shards, cap, rows, width)
    count = jnp.sum((owners == mine).astype(jnp.int32))
    state = jax.ShapeDtypeStruct((cap, width, width), f32)
    spec = slot_spec(width)
    piece = pl.BlockSpec((shards, 1, rows, width), lambda s: (0, s, 0, 0))
    cube = width * width * width
    hbm = pl.BlockSpec(memory_space=pl.ANY)
    vmem = pl.BlockSpec(memory_space=pltpu.VMEM)
    sems = pltpu.SemaphoreType.DMA((shards,))
    arrived, turned_old = pl.pallas_call(
        functools.partial(send_kernel, shards),
        in_specs=[hbm] * 4,
        out_specs=[hbm, vmem],
        out_shape=[jax.ShapeDtypeStruct(outgoing.shape, outgoing.dtype), state],
        scratch_shapes=[
            pltpu.VMEM((3, cap, width, width), f32),
            sems,
            sems,
            pltpu.SemaphoreType.DMA((3,)),
        ],
        compiler_params=pltpu.CompilerParams(collective_id=0, has_side_effects=True),
        name="send_step",
    )(outgoing, left_basis[0], right_basis[0], moment[0])
    smem = pl.BlockSpec(memory_space=pltpu.SMEM)
    update, left_new, right_new, moment_new, second_new, left_kept, right_kept = pl.pallas_call(
        slot_kernel,
        grid=(cap,),
        in_specs=[smem, piece] + [spec] * 7,
        out_specs=[piece] + [spec] * 6,
        out_shape=[jax.ShapeDtypeStruct((shards, cap, rows, width), f32)] + [state] * 6,
        cost_estimate=pl.CostEstimate(
            flops=26 * cap * cube, bytes_accessed=50 * cap * width * width, transcendentals=0
        ),
        name="slot_step",
    )(
        count.reshape(1),
        arrived,
        left_factor[0],
        right_factor[0],
        left_basis[0],
        right_basis[0],
        moment[0],
        second_moment[0],
        turned_old,
    )
    chosen = lax.dynamic_index_in_dim(rotation, mine, 0, keepdims=False)
    refreshed = (count > 0) & (group == chosen)
    size = width // 4 if width % 4 == 0 and width >= 256 else width
    head = pl.BlockSpec((1, width, width), lambda s: (0, 0, 0))
    one = jax.ShapeDtypeStruct((width, width), f32)
    returned, left_fresh, right_fresh = pl.pallas_call(
        functools.partial(return_kernel, shards, size, 4),
        grid=(1,),
        in_specs=[hbm] + [head] * 4,
        out_specs=[hbm] + [pl.BlockSpec((width, width), lambda s: (0, 0))] * 2,
        out_shape=[jax.ShapeDtypeStruct(update.shape, f32), one, one],
        scratch_shapes=[
            pltpu.VMEM((2, width, 2 * width), f32),
            pltpu.VMEM((2, width, width), f32),
            sems,
            sems,
        ],
        compiler_params=pltpu.CompilerParams(collective_id=1, has_side_effects=True),
        name="return_step",
    )(update, left_new, right_new, left_basis[0], right_basis[0])
    flag = refreshed.astype(jnp.int32).reshape(1)
    square = pl.BlockSpec((width, width), lambda s: (0, 0))
    left_basis_new, right_basis_new = pl.pallas_call(
        place_kernel,
        grid=(1,),
        in_specs=[smem, square, square, head, head],
        out_specs=[head] * 2,
        out_shape=[state] * 2,
        input_output_aliases={3: 0, 4: 1},
        name="place_step",
    )(flag, left_fresh, right_fresh, left_kept, right_kept)
    direction = jnp.take(returned.reshape(shards * cap, rows, width), target, axis=0)
    direction = direction.reshape(1, target.shape[0], rows * width)
    return (
        direction,
        left_new[None],
        right_new[None],
        left_basis_new[None],
        right_basis_new[None],
        moment_new[None],
        second_new[None],
    )


def solution(mesh):
    state = P("refresh", "fsdp", None, None)
    spread = P("refresh", None, "fsdp")
    in_specs = (spread, P("refresh", None, None), P()) + (state,) * 6
    out_specs = (spread,) + (state,) * 6
    return jax.shard_map(body, mesh=mesh, in_specs=in_specs, out_specs=out_specs, check_vma=False)
```

```python
import functools
import jax
import jax.numpy as jnp
from jax import lax
from jax.experimental import pallas as pl
from jax.experimental.pallas import tpu as pltpu
from jax.sharding import PartitionSpec as P

HIGHEST = lax.Precision.HIGHEST
EPSILON = 1e-08
NN = (((1,), (0,)), ((), ()))
TN = (((0,), (0,)), ((), ()))
NT = (((1,), (1,)), ((), ()))


def dot(a, b, dims):
    return lax.dot_general(a, b, dims, preferred_element_type=jnp.float32)


def exact(a, b, dims):
    return lax.dot_general(a, b, dims, precision=HIGHEST, preferred_element_type=jnp.float32)


def split(x):
    high = x.astype(jnp.bfloat16)
    return high, (x - high.astype(jnp.float32)).astype(jnp.bfloat16)


def dot3(a, b, dims):
    return dot(a[0], b[0], dims) + (dot(a[0], b[1], dims) + dot(a[1], b[0], dims))


def far_first(shards):
    return sorted(range(1, shards), key=lambda d: abs(2 * d - shards))


def greet(shards):
    me = lax.axis_index("fsdp")
    barrier = pltpu.get_barrier_semaphore()
    for d in range(1, shards):
        pl.semaphore_signal(
            barrier,
            inc=1,
            device_id={"fsdp": lax.rem(me + d, shards)},
            device_id_type=pl.DeviceIdType.MESH,
        )
    pl.semaphore_wait(barrier, shards - 1)


def eliminate(tiles, size, group):
    count = len(tiles)
    rows_of = lax.broadcasted_iota(jnp.int32, tiles[0][0].shape, 0)
    inverses = [[jnp.zeros_like(t) for t in tiles[0]] for _ in range(count)]
    for j in range(0, size, group):
        first = j // 8
        cols = []
        rows = []
        for m in range(count):
            cols.append(
                [
                    [
                        jnp.broadcast_to(t[:, j + k : j + k + 1], t.shape)
                        for t in tiles[m][first:]
                    ]
                    for k in range(group)
                ]
            )
            rows.append(
                [tiles[m][first][(j + k) % 8 : (j + k) % 8 + 1, :] for k in range(group)]
            )
        for k in range(group):
            s = (j + k) % 8
            for m in range(count):
                col = cols[m][k]
                inverse = 1.0 / col[0][s : s + 1, :]
                inverses[m][first] = jnp.where(rows_of == s, inverse, inverses[m][first])
                row = rows[m][k] * inverse
                below = [jnp.where(rows_of > s, col[0], 0.0)] + col[1:]
                for l in range(k + 1, group):
                    at = (j + l) % 8
                    entry = col[0][at : at + 1, :]
                    weight = entry * inverse
                    cols[m][l] = [c - b * weight for c, b in zip(cols[m][l], below)]
                    rows[m][l] = rows[m][l] - entry * row
                for n, b in enumerate(below):
                    tiles[m][first + n] = tiles[m][first + n] - b * row
    return tiles, inverses


def trade_kernel(
    shards,
    size,
    group,
    out_ref,
    lb_ref,
    rb_ref,
    moment_ref,
    second_ref,
    lf_ref,
    rf_ref,
    arrived_ref,
    turned_ref,
    returned_ref,
    lb_out,
    rb_out,
    state_ref,
    factor_ref,
    land_ref,
    rotated_ref,
    update_ref,
    work_ref,
    done_ref,
    send_sem,
    recv_sem,
    back_sem,
    home_sem,
    load_sem,
    store_sem,
):
    cap = land_ref.shape[1]
    rows = land_ref.shape[2]
    width = land_ref.shape[3]
    me = lax.axis_index("fsdp")
    loads = [
        pltpu.make_async_copy(ref, state_ref.at[i], load_sem.at[i])
        for i, ref in enumerate((lb_ref, moment_ref, rb_ref, second_ref))
    ]
    loads += [
        pltpu.make_async_copy(ref.at[0], factor_ref.at[i], load_sem.at[4 + i])
        for i, ref in enumerate((lf_ref, rf_ref))
    ]
    for load in loads:
        load.start()
    greet(shards)

    def copies_of(s, source, target, out_sem, in_sem):
        remote = []
        for d in far_first(shards):
            peer = lax.rem(me + d, shards)
            remote.append(
                pltpu.make_async_remote_copy(
                    src_ref=source.at[peer, s],
                    dst_ref=target.at[me, s],
                    send_sem=out_sem.at[d, s],
                    recv_sem=in_sem.at[d, s],
                    device_id={"fsdp": peer},
                    device_id_type=pl.DeviceIdType.MESH,
                )
            )
        local = pltpu.make_async_copy(source.at[me, s], target.at[me, s], out_sem.at[0, s])
        for copy in remote:
            copy.start()
        local.start()
        return remote, local

    sent = [copies_of(s, out_ref, land_ref, send_sem, recv_sem) for s in range(cap)]
    for load in loads:
        load.wait()
    lefts = [split(state_ref[0, s]) for s in range(cap)]
    rights = [split(state_ref[2, s]) for s in range(cap)]
    for s in range(cap):
        inner = dot3(lefts[s], split(state_ref[1, s]), TN)
        state_ref[1, s] = 0.9 * dot3(split(inner), rights[s], NN)
    back = []
    for s in range(cap):
        remote, local = sent[s]
        for copy in remote:
            copy.wait_recv()
        local.wait()
        block = land_ref[:, s].reshape(width, width)
        left = lefts[s]
        right = rights[s]
        inner = dot(left[0], block, TN) + dot(left[1], block, TN)
        turned = dot3(split(inner), right, NN)
        second_next = 0.95 * state_ref[3, s] + 0.05 * turned * turned
        scaled = (state_ref[1, s] + 0.1 * turned) / (jnp.sqrt(second_next) + EPSILON)
        backed = dot3(left, split(scaled), NN)
        update = dot3(split(backed), right, NT)
        update_ref[:, s] = update.reshape(shards, rows, width)
        rotated_ref[s] = turned
        back.append(copies_of(s, update_ref, returned_ref, back_sem, home_sem))
    stores = [
        pltpu.make_async_copy(land_ref, arrived_ref, store_sem.at[0]),
        pltpu.make_async_copy(rotated_ref, turned_ref, store_sem.at[1]),
    ]
    for store in stores:
        store.start()
    block = land_ref[:, 0].reshape(width, width)
    for m, (dims, at) in enumerate(((NT, 0), (TN, 2))):
        factor = 0.95 * factor_ref[m] + 0.05 / width * dot(block, block, dims)
        image = exact(factor, state_ref[at, 0], NN)
        flipped = image.T
        work_ref[m, :, :width] = exact(flipped, image, NN)
        work_ref[m, :, width:] = flipped
    lanes = 2 * size
    lane = lax.broadcasted_iota(jnp.int32, (size, lanes), 1)
    sub = lax.broadcasted_iota(jnp.int32, (size, lanes), 0)
    identity = jnp.where(lane == sub + size, 1.0, 0.0)
    for i in range(width // size):
        low = i * size
        start = low // lanes * lanes
        tiles = []
        for m in range(2):
            part = work_ref[m, low : low + size, start : start + lanes]
            if low != start:
                part = pltpu.roll(part, size, 1)
            both = jnp.where(lane < size, part, identity)
            tiles.append([both[8 * t : 8 * t + 8, :] for t in range(size // 8)])
        tiles, inverses = eliminate(tiles, size, group)
        for m in range(2):
            inverse_lower = jnp.concatenate(tiles[m], axis=0)[:, size:]
            inverse = jnp.concatenate(inverses[m], axis=0)
            inverse = jnp.concatenate([inverse] * (2 * width // lanes), axis=1)
            solved = exact(inverse_lower, work_ref[m, low : low + size, :], NN)
            done_ref[m, low : low + size, :] = solved[:, width:] * jnp.sqrt(inverse[:, width:])
            if low + size < width:
                trail = exact(solved[:, :width], solved * inverse, TN)
                work_ref[m, low + size :, :] -= trail[low + size :, :]
    lb_out[...] = done_ref[0].T
    rb_out[...] = done_ref[1].T
    for store in stores:
        store.wait()
    for remote, _ in sent:
        for copy in remote:
            copy.wait_send()
    for remote, local in back:
        for copy in remote:
            copy.wait()
        local.wait()


def write_kernel(
    target_ref,
    rotation_ref,
    arrived_ref,
    turned_ref,
    returned_ref,
    left_ref,
    right_ref,
    lf_ref,
    rf_ref,
    lb_ref,
    rb_ref,
    moment_ref,
    second_ref,
    direction_out,
    lf_out,
    rf_out,
    lb_out,
    rb_out,
    moment_out,
    second_out,
):
    cap = pl.num_programs(0)
    s = pl.program_id(0)
    width = lf_ref.shape[1]
    rows = returned_ref.shape[1]
    blocks = direction_out.shape[0]
    mine = lax.axis_index("fsdp")
    low = mine * cap

    def owned(b, total):
        at = target_ref[b]
        return total + jnp.where((at >= low) & (at < low + cap), 1, 0)

    live = s < lax.fori_loop(0, blocks, owned, 0)
    fresh = live & (s == 0) & (rotation_ref[mine] == lax.axis_index("refresh"))
    block = arrived_ref[:, 0].reshape(width, width)
    scale = 0.05 / width
    lf = lf_ref[0]
    rf = rf_ref[0]
    lf_out[0] = jnp.where(live, 0.95 * lf + scale * dot(block, block, NT), lf)
    rf_out[0] = jnp.where(live, 0.95 * rf + scale * dot(block, block, TN), rf)
    moment = moment_ref[0]
    moment_out[0] = jnp.where(live, 0.9 * moment + 0.1 * block.astype(jnp.float32), moment)
    second = second_ref[0]
    turned = turned_ref[0]
    second_out[0] = jnp.where(live, 0.95 * second + 0.05 * turned * turned, second)
    lb_out[0] = jnp.where(fresh, left_ref[...], lb_ref[0])
    rb_out[0] = jnp.where(fresh, right_ref[...], rb_ref[0])
    share = pl.cdiv(blocks, cap)

    def fetch(i, carry):
        b = jnp.minimum(s * share + i, blocks - 1)
        at = target_ref[b]
        for r in range(rows):
            direction_out[pl.ds(b, 1), r * width : (r + 1) * width] = returned_ref[at, r : r + 1, :]
        return carry

    lax.fori_loop(0, share, fetch, 0)


def slot_spec(width):
    return pl.BlockSpec((1, width, width), lambda s: (s, 0, 0))


def body(
    gradient,
    owner,
    rotation,
    left_factor,
    right_factor,
    left_basis,
    right_basis,
    moment,
    second_moment,
):
    shards = lax.axis_size("fsdp")
    cap = left_factor.shape[1]
    width = left_factor.shape[2]
    rows = width // shards
    f32 = jnp.float32
    owners = owner[0, :, 0]
    onehot = (owners[:, None] == jnp.arange(shards, dtype=jnp.int32)[None, :]).astype(jnp.int32)
    before = jnp.cumsum(onehot, axis=0) - onehot
    target = owners * cap + jnp.sum(before * onehot, axis=1)
    placing = (target[None, :] == jnp.arange(shards * cap, dtype=jnp.int32)[:, None]).astype(
        jnp.bfloat16
    )
    outgoing = jnp.dot(placing, gradient[0], preferred_element_type=f32).astype(jnp.bfloat16)
    outgoing = outgoing.reshape(shards, cap, rows, width)
    size = width // 4 if width % 4 == 0 and width >= 256 else width
    state = jax.ShapeDtypeStruct((cap, width, width), f32)
    one = jax.ShapeDtypeStruct((width, width), f32)
    hbm = pl.BlockSpec(memory_space=pl.ANY)
    vmem = pl.BlockSpec(memory_space=pltpu.VMEM)
    smem = pl.BlockSpec(memory_space=pltpu.SMEM)
    sems = pltpu.SemaphoreType.DMA((shards, cap))
    arrived, turned, returned, left_fresh, right_fresh = pl.pallas_call(
        functools.partial(trade_kernel, shards, size, 4),
        in_specs=[hbm] * 7,
        out_specs=[hbm] * 3 + [vmem] * 2,
        out_shape=[
            jax.ShapeDtypeStruct(outgoing.shape, outgoing.dtype),
            state,
            jax.ShapeDtypeStruct(outgoing.shape, f32),
            one,
            one,
        ],
        scratch_shapes=[
            pltpu.VMEM((4, cap, width, width), f32),
            pltpu.VMEM((2, width, width), f32),
            pltpu.VMEM(outgoing.shape, outgoing.dtype),
            pltpu.VMEM((cap, width, width), f32),
            pltpu.VMEM(outgoing.shape, f32),
            pltpu.VMEM((2, width, 2 * width), f32),
            pltpu.VMEM((2, width, width), f32),
            sems,
            sems,
            sems,
            sems,
            pltpu.SemaphoreType.DMA((6,)),
            pltpu.SemaphoreType.DMA((2,)),
        ],
        compiler_params=pltpu.CompilerParams(collective_id=0, has_side_effects=True),
        name="trade_step",
    )(
        outgoing,
        left_basis[0],
        right_basis[0],
        moment[0],
        second_moment[0],
        left_factor[0],
        right_factor[0],
    )
    spec = slot_spec(width)
    piece = pl.BlockSpec((shards, 1, rows, width), lambda s: (0, s, 0, 0))
    square = pl.BlockSpec((width, width), lambda s: (0, 0))
    blocks = target.shape[0]
    outs = pl.pallas_call(
        write_kernel,
        grid=(cap,),
        in_specs=[smem, smem, piece, spec]
        + [pl.BlockSpec((shards * cap, rows, width), lambda s: (0, 0, 0))]
        + [square] * 2
        + [spec] * 6,
        out_specs=[pl.BlockSpec((blocks, rows * width), lambda s: (0, 0))] + [spec] * 6,
        out_shape=[jax.ShapeDtypeStruct((blocks, rows * width), f32)] + [state] * 6,
        name="write_step",
    )(
        target,
        rotation,
        arrived,
        turned,
        returned.reshape(shards * cap, rows, width),
        left_fresh,
        right_fresh,
        left_factor[0],
        right_factor[0],
        left_basis[0],
        right_basis[0],
        moment[0],
        second_moment[0],
    )
    return tuple(out[None] for out in outs)


def solution(mesh):
    state = P("refresh", "fsdp", None, None)
    spread = P("refresh", None, "fsdp")
    in_specs = (spread, P("refresh", None, None), P()) + (state,) * 6
    out_specs = (spread,) + (state,) * 6
    return jax.shard_map(body, mesh=mesh, in_specs=in_specs, out_specs=out_specs, check_vma=False)
```

```python
import functools
import jax
import jax.numpy as jnp
from jax import lax
from jax.experimental import pallas as pl
from jax.experimental.pallas import tpu as pltpu
from jax.sharding import PartitionSpec as P

HIGHEST = lax.Precision.HIGHEST
EPSILON = 1e-08
NN = (((1,), (0,)), ((), ()))
TN = (((0,), (0,)), ((), ()))
NT = (((1,), (1,)), ((), ()))


def dot(a, b, dims):
    return lax.dot_general(a, b, dims, preferred_element_type=jnp.float32)


def exact(a, b, dims):
    return lax.dot_general(a, b, dims, precision=HIGHEST, preferred_element_type=jnp.float32)


def split(x):
    high = x.astype(jnp.bfloat16)
    return high, (x - high.astype(jnp.float32)).astype(jnp.bfloat16)


def dot3(a, b, dims):
    return dot(a[0], b[0], dims) + (dot(a[0], b[1], dims) + dot(a[1], b[0], dims))


def far_first(shards):
    return sorted(range(1, shards), key=lambda d: abs(2 * d - shards))


def greet(shards):
    me = lax.axis_index("fsdp")
    barrier = pltpu.get_barrier_semaphore()
    for d in range(1, shards):
        pl.semaphore_signal(
            barrier,
            inc=1,
            device_id={"fsdp": lax.rem(me + d, shards)},
            device_id_type=pl.DeviceIdType.MESH,
        )
    pl.semaphore_wait(barrier, shards - 1)


def eliminate(tiles, size, group):
    count = len(tiles)
    rows_of = lax.broadcasted_iota(jnp.int32, tiles[0][0].shape, 0)
    inverses = [[jnp.zeros_like(t) for t in tiles[0]] for _ in range(count)]
    for j in range(0, size, group):
        first = j // 8
        cols = []
        rows = []
        for m in range(count):
            cols.append(
                [
                    [
                        jnp.broadcast_to(t[:, j + k : j + k + 1], t.shape)
                        for t in tiles[m][first:]
                    ]
                    for k in range(group)
                ]
            )
            rows.append(
                [tiles[m][first][(j + k) % 8 : (j + k) % 8 + 1, :] for k in range(group)]
            )
        for k in range(group):
            s = (j + k) % 8
            for m in range(count):
                col = cols[m][k]
                inverse = 1.0 / col[0][s : s + 1, :]
                inverses[m][first] = jnp.where(rows_of == s, inverse, inverses[m][first])
                row = rows[m][k] * inverse
                below = [jnp.where(rows_of > s, col[0], 0.0)] + col[1:]
                for l in range(k + 1, group):
                    at = (j + l) % 8
                    entry = col[0][at : at + 1, :]
                    weight = entry * inverse
                    cols[m][l] = [c - b * weight for c, b in zip(cols[m][l], below)]
                    rows[m][l] = rows[m][l] - entry * row
                for n, b in enumerate(below):
                    tiles[m][first + n] = tiles[m][first + n] - b * row
    return tiles, inverses


def trade_kernel(
    shards,
    size,
    group,
    out_ref,
    lb_ref,
    rb_ref,
    moment_ref,
    second_ref,
    lf_ref,
    rf_ref,
    arrived_ref,
    turned_ref,
    returned_ref,
    lb_out,
    rb_out,
    state_ref,
    factor_ref,
    land_ref,
    rotated_ref,
    update_ref,
    work_ref,
    done_ref,
    send_sem,
    recv_sem,
    back_sem,
    home_sem,
    load_sem,
    store_sem,
):
    cap = land_ref.shape[1]
    rows = land_ref.shape[2]
    width = land_ref.shape[3]
    me = lax.axis_index("fsdp")
    loads = [
        pltpu.make_async_copy(ref, state_ref.at[i], load_sem.at[i])
        for i, ref in enumerate((lb_ref, moment_ref, rb_ref, second_ref))
    ]
    loads += [
        pltpu.make_async_copy(ref.at[0], factor_ref.at[i], load_sem.at[4 + i])
        for i, ref in enumerate((lf_ref, rf_ref))
    ]
    for load in loads:
        load.start()
    greet(shards)

    def copies_of(s, source, target, out_sem, in_sem):
        remote = []
        for d in far_first(shards):
            peer = lax.rem(me + d, shards)
            remote.append(
                pltpu.make_async_remote_copy(
                    src_ref=source.at[peer, s],
                    dst_ref=target.at[me, s],
                    send_sem=out_sem.at[d, s],
                    recv_sem=in_sem.at[d, s],
                    device_id={"fsdp": peer},
                    device_id_type=pl.DeviceIdType.MESH,
                )
            )
        local = pltpu.make_async_copy(source.at[me, s], target.at[me, s], out_sem.at[0, s])
        for copy in remote:
            copy.start()
        local.start()
        return remote, local

    sent = [copies_of(s, out_ref, land_ref, send_sem, recv_sem) for s in range(cap)]
    for load in loads:
        load.wait()
    lefts = [split(state_ref[0, s]) for s in range(cap)]
    rights = [split(state_ref[2, s]) for s in range(cap)]
    for s in range(cap):
        inner = dot3(lefts[s], split(state_ref[1, s]), TN)
        state_ref[1, s] = 0.9 * dot3(split(inner), rights[s], NN)
    back = []
    for s in range(cap):
        remote, local = sent[s]
        for copy in remote:
            copy.wait_recv()
        local.wait()
        block = land_ref[:, s].reshape(width, width)
        left = lefts[s]
        right = rights[s]
        inner = dot(left[0], block, TN) + dot(left[1], block, TN)
        turned = dot3(split(inner), right, NN)
        second_next = 0.95 * state_ref[3, s] + 0.05 * turned * turned
        scaled = (state_ref[1, s] + 0.1 * turned) / (jnp.sqrt(second_next) + EPSILON)
        backed = dot3(left, split(scaled), NN)
        update = dot3(split(backed), right, NT)
        update_ref[:, s] = update.reshape(shards, rows, width)
        rotated_ref[s] = turned
        back.append(copies_of(s, update_ref, returned_ref, back_sem, home_sem))
    stores = [
        pltpu.make_async_copy(land_ref, arrived_ref, store_sem.at[0]),
        pltpu.make_async_copy(rotated_ref, turned_ref, store_sem.at[1]),
    ]
    for store in stores:
        store.start()
    block = land_ref[:, 0].reshape(width, width)
    for m, (dims, at) in enumerate(((NT, 0), (TN, 2))):
        factor = 0.95 * factor_ref[m] + 0.05 / width * dot(block, block, dims)
        image = exact(factor, state_ref[at, 0], NN)
        flipped = image.T
        work_ref[m, :, :width] = exact(flipped, image, NN)
        work_ref[m, :, width:] = flipped
    lanes = 2 * size
    lane = lax.broadcasted_iota(jnp.int32, (size, lanes), 1)
    sub = lax.broadcasted_iota(jnp.int32, (size, lanes), 0)
    identity = jnp.where(lane == sub + size, 1.0, 0.0)
    for i in range(width // size):
        low = i * size
        start = low // lanes * lanes
        tiles = []
        for m in range(2):
            part = work_ref[m, low : low + size, start : start + lanes]
            if low != start:
                part = pltpu.roll(part, size, 1)
            both = jnp.where(lane < size, part, identity)
            tiles.append([both[8 * t : 8 * t + 8, :] for t in range(size // 8)])
        tiles, inverses = eliminate(tiles, size, group)
        for m in range(2):
            inverse_lower = jnp.concatenate(tiles[m], axis=0)[:, size:]
            inverse = jnp.concatenate(inverses[m], axis=0)
            inverse = jnp.concatenate([inverse] * (2 * width // lanes), axis=1)
            solved = exact(inverse_lower, work_ref[m, low : low + size, :], NN)
            done_ref[m, low : low + size, :] = solved[:, width:] * jnp.sqrt(inverse[:, width:])
            if low + size < width:
                trail = exact(solved[:, :width], solved * inverse, TN)
                work_ref[m, low + size :, :] -= trail[low + size :, :]
    lb_out[...] = done_ref[0].T
    rb_out[...] = done_ref[1].T
    for store in stores:
        store.wait()
    for remote, _ in sent:
        for copy in remote:
            copy.wait_send()
    for remote, local in back:
        for copy in remote:
            copy.wait()
        local.wait()


def write_kernel(
    target_ref,
    rotation_ref,
    arrived_ref,
    turned_ref,
    returned_ref,
    left_ref,
    right_ref,
    lf_ref,
    rf_ref,
    lb_ref,
    rb_ref,
    moment_ref,
    second_ref,
    direction_out,
    lf_out,
    rf_out,
    lb_out,
    rb_out,
    moment_out,
    second_out,
):
    cap = pl.num_programs(0)
    s = pl.program_id(0)
    width = lf_ref.shape[1]
    rows = returned_ref.shape[1]
    blocks = direction_out.shape[0]
    mine = lax.axis_index("fsdp")
    low = mine * cap

    def owned(b, total):
        at = target_ref[b]
        return total + jnp.where((at >= low) & (at < low + cap), 1, 0)

    live = s < lax.fori_loop(0, blocks, owned, 0)
    fresh = live & (s == 0) & (rotation_ref[mine] == lax.axis_index("refresh"))
    block = arrived_ref[:, 0].reshape(width, width)
    scale = 0.05 / width
    lf = lf_ref[0]
    rf = rf_ref[0]
    lf_out[0] = jnp.where(live, 0.95 * lf + scale * dot(block, block, NT), lf)
    rf_out[0] = jnp.where(live, 0.95 * rf + scale * dot(block, block, TN), rf)
    moment = moment_ref[0]
    moment_out[0] = jnp.where(live, 0.9 * moment + 0.1 * block.astype(jnp.float32), moment)
    second = second_ref[0]
    turned = turned_ref[0]
    second_out[0] = jnp.where(live, 0.95 * second + 0.05 * turned * turned, second)
    lb_out[0] = jnp.where(fresh, left_ref[...], lb_ref[0])
    rb_out[0] = jnp.where(fresh, right_ref[...], rb_ref[0])
    share = pl.cdiv(blocks, cap)

    def fetch(i, carry):
        b = jnp.minimum(s * share + i, blocks - 1)
        at = target_ref[b]
        for r in range(rows):
            direction_out[pl.ds(b, 1), r * width : (r + 1) * width] = returned_ref[at, r : r + 1, :]
        return carry

    lax.fori_loop(0, share, fetch, 0)


def slot_spec(width):
    return pl.BlockSpec((1, width, width), lambda s: (s, 0, 0))


def body(
    gradient,
    owner,
    rotation,
    left_factor,
    right_factor,
    left_basis,
    right_basis,
    moment,
    second_moment,
):
    shards = lax.axis_size("fsdp")
    cap = left_factor.shape[1]
    width = left_factor.shape[2]
    rows = width // shards
    f32 = jnp.float32
    owners = owner[0, :, 0]
    onehot = (owners[:, None] == jnp.arange(shards, dtype=jnp.int32)[None, :]).astype(jnp.int32)
    before = jnp.cumsum(onehot, axis=0) - onehot
    target = owners * cap + jnp.sum(before * onehot, axis=1)
    placing = (target[None, :] == jnp.arange(shards * cap, dtype=jnp.int32)[:, None]).astype(
        jnp.bfloat16
    )
    outgoing = jnp.dot(placing, gradient[0], preferred_element_type=f32).astype(jnp.bfloat16)
    outgoing = outgoing.reshape(shards, cap, rows, width)
    size = width // 4 if width % 4 == 0 and width >= 256 else width
    state = jax.ShapeDtypeStruct((cap, width, width), f32)
    one = jax.ShapeDtypeStruct((width, width), f32)
    hbm = pl.BlockSpec(memory_space=pl.ANY)
    vmem = pl.BlockSpec(memory_space=pltpu.VMEM)
    smem = pl.BlockSpec(memory_space=pltpu.SMEM)
    sems = pltpu.SemaphoreType.DMA((shards, cap))
    arrived, turned, returned, left_fresh, right_fresh = pl.pallas_call(
        functools.partial(trade_kernel, shards, size, 4),
        in_specs=[pl.BlockSpec(memory_space=pltpu.HBM)] * 7,
        out_specs=[hbm] * 3 + [vmem] * 2,
        out_shape=[
            jax.ShapeDtypeStruct(outgoing.shape, outgoing.dtype),
            state,
            jax.ShapeDtypeStruct(outgoing.shape, f32),
            one,
            one,
        ],
        scratch_shapes=[
            pltpu.VMEM((4, cap, width, width), f32),
            pltpu.VMEM((2, width, width), f32),
            pltpu.VMEM(outgoing.shape, outgoing.dtype),
            pltpu.VMEM((cap, width, width), f32),
            pltpu.VMEM(outgoing.shape, f32),
            pltpu.VMEM((2, width, 2 * width), f32),
            pltpu.VMEM((2, width, width), f32),
            sems,
            sems,
            sems,
            sems,
            pltpu.SemaphoreType.DMA((6,)),
            pltpu.SemaphoreType.DMA((2,)),
        ],
        compiler_params=pltpu.CompilerParams(
            collective_id=0, has_side_effects=True, vmem_limit_bytes=24 << 20
        ),
        name="trade_step",
    )(
        outgoing,
        *(
            pltpu.with_memory_space_constraint(x[0], pltpu.HBM)
            for x in (left_basis, right_basis, moment, second_moment, left_factor, right_factor)
        ),
    )
    spec = slot_spec(width)
    piece = pl.BlockSpec((shards, 1, rows, width), lambda s: (0, s, 0, 0))
    square = pl.BlockSpec((width, width), lambda s: (0, 0))
    blocks = target.shape[0]
    outs = pl.pallas_call(
        write_kernel,
        grid=(cap,),
        in_specs=[smem, smem, piece, spec]
        + [pl.BlockSpec((shards * cap, rows, width), lambda s: (0, 0, 0))]
        + [square] * 2
        + [spec] * 6,
        out_specs=[pl.BlockSpec((blocks, rows * width), lambda s: (0, 0))] + [spec] * 6,
        out_shape=[jax.ShapeDtypeStruct((blocks, rows * width), f32)] + [state] * 6,
        compiler_params=pltpu.CompilerParams(vmem_limit_bytes=20 << 20),
        name="write_step",
    )(
        target,
        rotation,
        arrived,
        turned,
        returned.reshape(shards * cap, rows, width),
        left_fresh,
        right_fresh,
        left_factor[0],
        right_factor[0],
        left_basis[0],
        right_basis[0],
        moment[0],
        second_moment[0],
    )
    return tuple(out[None] for out in outs)


def solution(mesh):
    state = P("refresh", "fsdp", None, None)
    spread = P("refresh", None, "fsdp")
    in_specs = (spread, P("refresh", None, None), P()) + (state,) * 6
    out_specs = (spread,) + (state,) * 6
    return jax.shard_map(body, mesh=mesh, in_specs=in_specs, out_specs=out_specs, check_vma=False)
```
